32 devices in a mesh: space: 16 (over z, x, core), batch: 2 (over y).
Axes of the slice: x: 2, y: 2, z: 4, core: 2. Of those that a mesh axis runs over, the one named last changes fastest.
Arguments:
- fine_parts: bfloat16 [2, 8192, 128], P('batch', 'space'), may hold values from -6 to 6
- parent_parts: bfloat16 [2, 1024, 128], P('batch', 'space'), may hold values from -6 to 6
- coarse_local: float32 [1024, 128], P('space'), may hold values from -6 to 6
- fine_source: int32 [189, 8192], P(None, 'space'), may hold values from 0 to 159
- fine_operator: int32 [189, 8192], P(None, 'space'), may hold values from 0 to 63
- parent_source: int32 [189, 1024], P(None, 'space'), may hold values from 0 to 159
- parent_operator: int32 [189, 1024], P(None, 'space'), may hold values from 0 to 63
- operators: bfloat16 [64, 128, 128], replicated, may hold values from -0.0390625 to 0.0390625
- child_shift: bfloat16 [8, 128, 128], replicated, may hold values from -0.5 to 0.5
- basis: bfloat16 [8192, 32, 128], P('space', 'batch'), may hold values from -0.5 to 0.5
- counts: int32 [2, 8192], P('batch', 'space'), may hold values from 1 to 16
Outputs:
- potential: float32 [32, 8192], P('batch', 'space')
The draws below stay inside these ranges and needn't reach their ends.
Inputs may be any that keep to these rules, and one draw needn't show every extreme that they name: `fine_source`: an entry v names, in the target's own block if v // 32 is 0 and else in the block whose index differs from the target's in bit v // 32 - 1, box v % 32 of the aligned group of 32 boxes that holds the target's position. `parent_source`: an entry v names, in the target's own block if v // 32 is 0 and else in the block whose index differs from the target's in bit v // 32 - 1, parent box v % 32 of the aligned group of 32 parent boxes that holds the target's position.
All inputs are finite; a program needn't handle non-finite values.
Results may differ from the reference program's by a relative error of at most 0.015.
Values may be sent and summed in bfloat16 or wider, within the bound.
No kernel may reach another device: no remote copies, remote signals or barrier semaphores. Data moves between devices by JAX's collectives and lax.ppermute only.
A program may use at most 64 MiB of HBM per device.

```python
import math
import jax
import jax.numpy as jnp
from jax import lax

NC = 128
NTERMS = 121
NI = 189
NOPS = 64
BOX_DEV = 512
SLOT_DEV = 16
PB_DEV = 64
WINDOW = 32
NBATCH = 2
NBOX = 8192
PNBOX = 1024
SLOTS = 32


def with_ends(drawn, own_key, low, high):
    extent = drawn.shape
    place = [jax.random.randint(jax.random.fold_in(own_key, axis), (), 0, extent[axis]) for axis in range(len(extent))]
    drawn = drawn.at[tuple(place)].set(low)
    longest = extent.index(max(extent))
    place[longest] = (place[longest] + 1) % extent[longest]
    return drawn.at[tuple(place)].set(high)


def level_of(own_key, shape, split, low, high):
    loudness = 1.0
    for position, shards_of in split:
        heights = jax.random.uniform(jax.random.fold_in(jax.random.fold_in(own_key, 6), position), (shards_of,), jnp.float32, low / len(split), high / len(split))
        loudness = loudness * jnp.repeat(jnp.exp(heights), shape[position] // shards_of).reshape((-1,) + (1,) * (len(shape) - 1 - position))
    return loudness


def centred(stream_key, shape, scale, limit, split=(), kind=jnp.bfloat16):
    entries = scale * jax.random.normal(stream_key, shape, jnp.float32)
    if split:
        entries = entries * level_of(stream_key, shape, split, -0.22, 0.18)
    return jnp.clip(entries, -limit, limit).astype(kind)


def setup_inputs(seed: int = 0) -> dict:
    streams_of = jax.random.split(jax.random.key(seed), 12)
    return {
        "fine_parts": centred(streams_of[0], (NBATCH, NBOX, NC), (1.0 / NBATCH ** 0.5), 6.0, ((0, 2), (1, 16))),
        "parent_parts": centred(streams_of[1], (NBATCH, PNBOX, NC), (1.0 / NBATCH ** 0.5), 6.0, ((0, 2), (1, 16))),
        "coarse_local": centred(streams_of[2], (PNBOX, NC), 1.0, 6.0, ((0, 16),), jnp.float32),
        "fine_source": with_ends(jax.random.randint(streams_of[3], (NI, NBOX), 0, 5 * WINDOW), jax.random.fold_in(streams_of[3], 1), 0, (5 * WINDOW) - 1).astype(jnp.int32),
        "fine_operator": with_ends(jax.random.randint(streams_of[4], (NI, NBOX), 0, NOPS), jax.random.fold_in(streams_of[4], 1), 0, NOPS - 1).astype(jnp.int32),
        "parent_source": with_ends(jax.random.randint(streams_of[5], (NI, PNBOX), 0, 5 * WINDOW), jax.random.fold_in(streams_of[5], 1), 0, (5 * WINDOW) - 1).astype(jnp.int32),
        "parent_operator": with_ends(jax.random.randint(streams_of[6], (NI, PNBOX), 0, NOPS), jax.random.fold_in(streams_of[6], 1), 0, NOPS - 1).astype(jnp.int32),
        "operators": centred(streams_of[7], (NOPS, NC, NC), (NC * NI) ** -0.5, 0.0390625),
        "child_shift": centred(streams_of[8], (8, NC, NC), NC ** -0.5, 0.5),
        "basis": centred(streams_of[9], (NBOX, SLOTS, NC), NTERMS ** -0.5, 0.5, ((0, 16), (1, 2))),
        "counts": with_ends(jax.random.randint(streams_of[10], (NBATCH, NBOX), 1, SLOT_DEV + 1), jax.random.fold_in(streams_of[10], 1), 1, SLOT_DEV).astype(jnp.int32),
    }


def far_field(multipole, source_list, operator_list, block_rows, operators):
    total_rows, coef_width = multipole.shape
    kind_count = operators.shape[0]
    list_length = source_list.shape[0]
    box_index = jnp.arange(total_rows, dtype=jnp.int32)
    owner_block = (box_index // block_rows)[None, :]
    group_start = ((box_index % block_rows) // WINDOW * WINDOW)[None, :]
    which_block = source_list // WINDOW
    flipped = jnp.bitwise_xor(owner_block, jnp.left_shift(jnp.ones_like(which_block), jnp.maximum(which_block - 1, 0)))
    home_block = jnp.where(which_block == 0, owner_block, flipped)
    global_source = (home_block * block_rows + group_start + source_list % WINDOW).astype(jnp.int32)
    flat_ops = operators.reshape(kind_count * coef_width, coef_width)
    piece_rows = math.gcd(total_rows, 256)
    piece_count = total_rows // piece_rows
    source_pieces = global_source.reshape(list_length, piece_count, piece_rows).transpose(1, 0, 2)
    kind_pieces = operator_list.reshape(list_length, piece_count, piece_rows).transpose(1, 0, 2)
    kinds_iota = jnp.arange(kind_count, dtype=jnp.int32)

    def one_piece(pieces):
        sources, kinds = pieces
        gathered = multipole[sources].astype(jnp.float32)
        onehot = (kinds[:, :, None] == kinds_iota).astype(jnp.float32)
        grouped = jnp.einsum("jbt,jbk->btk", onehot, gathered).astype(jnp.bfloat16)
        return jnp.dot(grouped.reshape(piece_rows, kind_count * coef_width), flat_ops, preferred_element_type=jnp.float32)

    return lax.map(one_piece, (source_pieces, kind_pieces)).reshape(total_rows, coef_width)


def reference(fine_parts, parent_parts, coarse_local, fine_source, fine_operator, parent_source, parent_operator, operators, child_shift, basis, counts):
    fine_mult = jnp.sum(fine_parts.astype(jnp.float32), axis=0).astype(jnp.bfloat16)
    parent_mult = jnp.sum(parent_parts.astype(jnp.float32), axis=0).astype(jnp.bfloat16)
    fine_far = far_field(fine_mult, fine_source, fine_operator, BOX_DEV, operators)
    parent_far = far_field(parent_mult, parent_source, parent_operator, PB_DEV, operators)
    parent_local = (coarse_local + parent_far).astype(jnp.bfloat16)
    shifted = jnp.einsum("pk,okl->pol", parent_local.astype(jnp.float32), child_shift.astype(jnp.float32)).reshape(fine_far.shape)
    coef_width = fine_far.shape[1]
    keep = jnp.arange(coef_width, dtype=jnp.int32) < NTERMS
    local = jnp.where(keep[None, :], shifted + fine_far, 0.0).astype(jnp.bfloat16)
    total_rows = local.shape[0]
    piece_rows = math.gcd(total_rows, 256)
    piece_count = total_rows // piece_rows
    basis_pieces = basis.reshape(piece_count, piece_rows, basis.shape[1], basis.shape[2])
    local_pieces = local.reshape(piece_count, piece_rows, coef_width)

    def evaluate(pieces):
        block_basis, block_local = pieces
        return jnp.einsum("bsk,bk->bs", block_basis.astype(jnp.float32), block_local.astype(jnp.float32))

    values = lax.map(evaluate, (basis_pieces, local_pieces)).reshape(total_rows, basis.shape[1]).T
    slot_index = jnp.arange(values.shape[0], dtype=jnp.int32)[:, None] % SLOT_DEV
    limits = jnp.repeat(counts, SLOT_DEV, axis=0)
    return jnp.where(slot_index < limits, values, 0.0)
```

```python
import functools

import jax
import jax.numpy as jnp
from jax import lax
from jax.experimental import pallas as pl
from jax.experimental.pallas import tpu as pltpu
from jax.sharding import PartitionSpec as P

NTERMS = 121
WINDOW = 32
LANES = 128
VMEM = pl.BlockSpec(memory_space=pltpu.VMEM)
SMEM = pl.BlockSpec(memory_space=pltpu.SMEM)


def round_up(value, step):
    return -(-value // step) * step


def rotate(value, axis, step):
    size = lax.axis_size(axis)
    return lax.ppermute(value, axis, [(i, (i + step) % size) for i in range(size)])


def partner(value, axis, apart):
    return lax.ppermute(value, axis, [(i, i ^ 1 << apart) for i in range(lax.axis_size(axis))])


def count_kernel(
    widths, kinds, columns, member_ref, fs_ref, fo_ref, ps_ref, po_ref, out_ref, *scratch
):
    member = member_ref[0]
    depth = scratch[0].shape[1]
    half = jnp.bfloat16
    rows_iota = lax.broadcasted_iota(jnp.int32, (16, depth), 0).astype(half)
    one = jnp.ones((), half)
    zero = jnp.zeros((), half)

    def hot(row_ref, row, size):
        values = jnp.broadcast_to(row_ref[pl.ds(row, 1), :], (16, depth)).astype(half)
        pieces = [jnp.where(values == rows_iota + 16 * k, one, zero) for k in range(size // 16)]
        return jnp.concatenate(pieces, 0).astype(jnp.float8_e4m3fn)

    done = 0
    for (source_ref, kind_ref), (source_rows, kind_rows), width in zip(
        ((fs_ref, fo_ref), (ps_ref, po_ref)), (scratch[:2], scratch[2:]), widths
    ):
        length, total = source_ref.shape
        whole = length // 8 * 8
        span = width if width % LANES == 0 else total
        offset = 0 if span == width else member * width
        for ref, rows in ((source_ref, source_rows), (kind_ref, kind_rows)):
            if span == total:
                body, tail = ref[:whole, :], ref[whole:, :]
            else:
                lanes = pl.ds(pl.multiple_of(member * width, LANES), width)
                body, tail = ref[:whole, lanes], ref[whole:, lanes]
            pad = jnp.full((depth - length, span), -1, jnp.int32)
            entries = jnp.concatenate([body, tail, pad], 0).astype(jnp.float32)
            extra = rows.shape[0] - span
            if extra:
                entries = jnp.concatenate([entries, jnp.zeros((depth, extra), jnp.float32)], 1)
            rows[...] = entries.T

        def one_box(box, _, offset=offset, done=done, source_rows=source_rows, kind_rows=kind_rows):
            source_hot = hot(source_rows, box + offset, columns)
            kind_hot = hot(kind_rows, box + offset, kinds)
            counted = lax.dot_general(
                kind_hot, source_hot, (((1,), (1,)), ((), ())), preferred_element_type=jnp.float32
            )
            start = pl.multiple_of((box + done) * kinds, kinds)
            out_ref[pl.ds(start, kinds), :] = counted.astype(half)
            return 0

        lax.fori_loop(0, width, one_box, 0, unroll=8)
        done += width


def count_entries(member, fine_source, fine_kind, parent_source, parent_kind, widths, kinds, columns):
    length = fine_source.shape[0]
    depth = round_up(length, LANES)
    boxes = sum(widths)
    scratch = []
    for source, width in ((fine_source, widths[0]), (parent_source, widths[1])):
        span = width if width % LANES == 0 else source.shape[1]
        scratch += [pltpu.VMEM((round_up(span, LANES), depth), jnp.float32)] * 2
    return pl.pallas_call(
        functools.partial(count_kernel, widths, kinds, columns),
        out_shape=jax.ShapeDtypeStruct((boxes * kinds, columns), jnp.bfloat16),
        in_specs=[SMEM] + [VMEM] * 4,
        out_specs=VMEM,
        scratch_shapes=scratch,
        compiler_params=pltpu.CompilerParams(vmem_limit_bytes=24 << 20),
        cost_estimate=pl.CostEstimate(
            flops=2 * boxes * depth * kinds * columns * 4,
            bytes_accessed=boxes * kinds * columns * 2,
            transcendentals=0,
        ),
        name="counts",
    )(member, fine_source, fine_kind, parent_source, parent_kind)


def local_kernel(
    widths, kinds, member_ref, count_ref, *refs
):
    (b0, b1, b2, b3, b4, ops_ref, coarse_ref, shift_ref, out_ref, grouped, total, moved) = refs
    blocks = (b0, b1, b2, b3, b4)
    member = member_ref[0]
    fine, parent = widths
    coef = out_ref.shape[1]
    rows = WINDOW * kinds

    def one_window(window, _):
        start = pl.multiple_of(window * WINDOW, WINDOW)
        nearby = jnp.concatenate([ref[pl.ds(start, WINDOW), :] for ref in blocks], 0)
        at = pl.multiple_of(window * rows, rows)
        grouped[pl.ds(at, rows), :] = jnp.dot(
            count_ref[pl.ds(at, rows), :], nearby, preferred_element_type=jnp.float32
        )
        return 0

    lax.fori_loop(0, fine // WINDOW, one_window, 0)
    spread = max(parent, WINDOW)
    for piece in range(spread // WINDOW):
        start = fine + piece * WINDOW
        nearby = jnp.concatenate([ref[start : start + WINDOW, :] for ref in blocks], 0)
        count = min(parent, WINDOW) * kinds
        at = (fine + piece * WINDOW) * kinds
        grouped[at : at + count, :] = jnp.dot(
            count_ref[at : at + count, :], nearby, preferred_element_type=jnp.float32
        )

    boxes = fine + parent
    step = 8
    total[...] = jnp.zeros_like(total)

    def some_kinds(at, _):
        picked = [
            grouped[pl.ds(at * step + k, boxes, stride=kinds), :].astype(jnp.bfloat16)
            for k in range(step)
        ]
        start = pl.multiple_of(at * step * coef, step * coef)
        total[...] += jnp.dot(
            jnp.concatenate(picked, 1),
            ops_ref[pl.ds(start, step * coef), :],
            preferred_element_type=jnp.float32,
        )
        return 0

    lax.fori_loop(0, kinds // step, some_kinds, 0)
    begin = member * parent
    if parent % 8 == 0:
        begin = pl.multiple_of(begin, 8)
    parent_local = coarse_ref[pl.ds(begin, parent), :] + total[fine:, :]
    parent_local = parent_local.astype(jnp.bfloat16)
    octants = shift_ref.shape[0]
    for octant in range(octants):
        moved[pl.ds(octant, parent, stride=octants), :] = jnp.dot(
            parent_local, shift_ref[octant], preferred_element_type=jnp.float32
        )
    whole = moved[...] + total[:fine, :]
    keep = lax.broadcasted_iota(jnp.int32, whole.shape, 1) < NTERMS
    out_ref[...] = jnp.where(keep, whole, 0.0).astype(jnp.bfloat16)


def local_of(member, counted, blocks, flat_ops, coarse, child_shift, widths, kinds):
    fine, parent = widths
    coef = flat_ops.shape[1]
    boxes = fine + parent
    return pl.pallas_call(
        functools.partial(local_kernel, widths, kinds),
        out_shape=jax.ShapeDtypeStruct((fine, coef), jnp.bfloat16),
        in_specs=[SMEM] + [VMEM] * 9,
        out_specs=VMEM,
        scratch_shapes=[
            pltpu.VMEM((boxes * kinds, coef), jnp.float32),
            pltpu.VMEM((boxes, coef), jnp.float32),
            pltpu.VMEM((fine, coef), jnp.float32),
        ],
        compiler_params=pltpu.CompilerParams(vmem_limit_bytes=32 << 20),
        cost_estimate=pl.CostEstimate(
            flops=8 * boxes * kinds * coef * 256,
            bytes_accessed=boxes * kinds * coef * 4,
            transcendentals=0,
        ),
        name="far",
    )(member, counted, *blocks, flat_ops, coarse, child_shift)


def slots_of(basis_ref, counts_ref, box, local):
    count, coef = local.shape
    slots = basis_ref.shape[1]
    pairs = count // 2
    odd = lax.broadcasted_iota(jnp.int32, local.shape, 0) % 2
    zero = jnp.zeros_like(local)
    right = jnp.concatenate(
        [jnp.where(odd == 0, local, zero), jnp.where(odd == 1, local, zero)], 1
    )
    left = basis_ref[pl.ds(box, count)].reshape(pairs, 2, slots, coef)
    left = jnp.concatenate([left[:, 0], left[:, 1]], 2).reshape(pairs * slots, 2 * coef)
    values = lax.dot_general(
        left, right, (((1,), (1,)), ((), ())), preferred_element_type=jnp.float32
    ).reshape(pairs, slots, count)
    lane = lax.broadcasted_iota(jnp.int32, (slots, count), 1) // 2
    summed = jnp.zeros((slots, count), jnp.float32)
    for pair in range(pairs):
        summed += jnp.where(lane == pair, values[pair], 0.0)
    slot = lax.broadcasted_iota(jnp.int32, summed.shape, 0)
    limit = counts_ref[:, pl.ds(box, count)]
    return jnp.where(slot < limit, summed, 0.0)


def own_kernel(member_ref, local_ref, basis_ref, counts_ref, out_ref):
    width = local_ref.shape[0]
    for piece in range(width // LANES):
        box = pl.multiple_of(member_ref[0] * width + piece * LANES, LANES)
        at = slice(piece * LANES, (piece + 1) * LANES)
        out_ref[:, at] = slots_of(basis_ref, counts_ref, box, local_ref[at, :])


def other_kernel(member_ref, local_ref, basis_ref, counts_ref, own_ref, out_ref):
    width = local_ref.shape[0]
    out_ref[:, pl.ds(pl.multiple_of(member_ref[0] * width, LANES), width)] = own_ref[...]
    for piece in range(width // LANES):
        box = pl.multiple_of((1 - member_ref[0]) * width + piece * LANES, LANES)
        at = slice(piece * LANES, (piece + 1) * LANES)
        out_ref[:, pl.ds(box, LANES)] = slots_of(basis_ref, counts_ref, box, local_ref[at, :])


def evaluate(kernel, columns, member, local, basis, counts, *more):
    slots = basis.shape[1]
    return pl.pallas_call(
        kernel,
        out_shape=jax.ShapeDtypeStruct((slots, columns), jnp.float32),
        in_specs=[SMEM] + [VMEM] * (3 + len(more)),
        out_specs=VMEM,
        compiler_params=pltpu.CompilerParams(vmem_limit_bytes=16 << 20),
        cost_estimate=pl.CostEstimate(
            flops=2 * local.shape[0] * slots * 256 * 128,
            bytes_accessed=local.shape[0] * slots * 256,
            transcendentals=0,
        ),
        name="slots",
    )(member, local, basis, counts, *more)


def body(
    fine_parts,
    parent_parts,
    coarse_local,
    fine_source,
    fine_operator,
    parent_source,
    parent_operator,
    operators,
    child_shift,
    basis,
    counts,
):
    group = lax.axis_size("batch")
    member = lax.axis_index("batch")
    kinds, coef, _ = operators.shape
    fine_total, parent_total = fine_source.shape[1], parent_source.shape[1]
    widths = (fine_total // group, parent_total // group)
    index = member.astype(jnp.int32).reshape(1)

    def share(whose):
        fine_size, parent_size = max(widths[0], WINDOW), max(widths[1], WINDOW)
        fine_at = whose * widths[0] // WINDOW * WINDOW
        parent_at = whose * widths[1] // WINDOW * WINDOW
        return jnp.concatenate(
            [
                lax.dynamic_slice_in_dim(fine_parts[0], fine_at, fine_size, 0),
                lax.dynamic_slice_in_dim(parent_parts[0], parent_at, parent_size, 0),
            ],
            0,
        )

    summed = share(member).astype(jnp.float32)
    for step in range(1, group):
        summed += rotate(share((member + step) % group), "batch", step).astype(jnp.float32)
    own = summed.astype(jnp.bfloat16)
    blocks = [own] + [partner(own, "space", bit) for bit in range(4)]
    counted = count_entries(
        index,
        fine_source,
        fine_operator,
        parent_source,
        parent_operator,
        widths,
        kinds,
        5 * WINDOW,
    )
    local = local_of(
        index,
        counted,
        blocks,
        operators.reshape(kinds * coef, coef),
        coarse_local,
        child_shift,
        widths,
        kinds,
    )
    if group == 2 and widths[0] % LANES == 0:
        other = rotate(local, "batch", 1)
        mine = evaluate(own_kernel, widths[0], index, local, basis, counts)
        return evaluate(other_kernel, fine_total, index, other, basis, counts, mine)
    gathered = jnp.zeros((fine_total, coef), local.dtype)
    for step in range(group):
        piece = rotate(local, "batch", step) if step else local
        at = (member - step) % group * widths[0]
        gathered = lax.dynamic_update_slice_in_dim(gathered, piece, at, 0)
    return evaluate(own_kernel, fine_total, index * 0, gathered, basis, counts)


def solution(mesh):
    placed = (
        P("batch", "space", None),
        P("batch", "space", None),
        P("space", None),
        P(None, "space"),
        P(None, "space"),
        P(None, "space"),
        P(None, "space"),
        P(),
        P(),
        P("space", "batch", None),
        P("batch", "space"),
    )
    return jax.shard_map(
        body, mesh=mesh, in_specs=placed, out_specs=P("batch", "space"), check_vma=False
    )
```

```python
import functools

import jax
import jax.numpy as jnp
from jax import lax
from jax.experimental import pallas as pl
from jax.experimental.pallas import tpu as pltpu
from jax.sharding import PartitionSpec as P

NTERMS = 121
WINDOW = 32
LANES = 128
VMEM = pl.BlockSpec(memory_space=pltpu.VMEM)
SMEM = pl.BlockSpec(memory_space=pltpu.SMEM)


def round_up(value, step):
    return -(-value // step) * step


def rotate(value, axis, step):
    size = lax.axis_size(axis)
    return lax.ppermute(value, axis, [(i, (i + step) % size) for i in range(size)])


def partner(value, axis, apart):
    return lax.ppermute(value, axis, [(i, i ^ 1 << apart) for i in range(lax.axis_size(axis))])


def pack_kernel(widths, member_ref, fine_ref, parent_ref, *refs):
    lists, outs, sem = refs[:4], refs[4:-1], refs[-1]
    member = member_ref[0]
    fine, parent = widths
    copies = []
    for at, out in ((member, outs[0]), (1 - member, outs[1])):
        for ref, width, row in ((fine_ref, fine, 0), (parent_ref, parent, fine)):
            start = pl.multiple_of(at * width, WINDOW)
            copies.append((ref.at[0, pl.ds(start, width), :], out.at[pl.ds(row, width), :]))
    lanes = pl.ds(pl.multiple_of(member * fine, LANES), fine)
    copies += [(ref.at[:, lanes], out) for ref, out in zip(lists[:2], outs[2:4])]
    boxes = pl.ds(pl.multiple_of(member * parent, 8), parent)
    copies += [(ref.at[boxes, :], out) for ref, out in zip(lists[2:], outs[4:])]
    copies = [pltpu.make_async_copy(*pair, sem.at[i]) for i, pair in enumerate(copies)]
    for copy in copies:
        copy.start()
    for copy in copies:
        copy.wait()


def pack(member, fine_parts, parent_parts, lists, widths):
    in_place = pl.BlockSpec(memory_space=pltpu.HBM)
    length = lists[0].shape[0]
    coef = fine_parts.shape[2]
    chunk = jax.ShapeDtypeStruct((sum(widths), coef), fine_parts.dtype)
    mine = jax.ShapeDtypeStruct((length, widths[0]), jnp.int32)
    parents = jax.ShapeDtypeStruct((widths[1], length), jnp.int32)
    shapes = [chunk, chunk, mine, mine, parents, parents]
    return pl.pallas_call(
        functools.partial(pack_kernel, widths),
        out_shape=shapes,
        in_specs=[SMEM] + [in_place] * 6,
        out_specs=[VMEM] * 6,
        scratch_shapes=[pltpu.SemaphoreType.DMA((8,))],
        compiler_params=pltpu.CompilerParams(vmem_limit_bytes=4 << 20),
        name="pack",
    )(
        member,
        *(
            pltpu.with_memory_space_constraint(each, pltpu.HBM)
            for each in (fine_parts, parent_parts, *lists)
        ),
    )


def count_kernel(levels, kinds, columns, *refs):
    lists, out_ref, scratch = refs[: 2 * len(levels)], refs[-1 - 2 * len(levels)], refs[-2 * len(levels) :]
    depth = scratch[0].shape[1]
    half, quarter = jnp.bfloat16, jnp.float8_e4m3fn
    rows_iota = lax.broadcasted_iota(jnp.int32, (32, depth), 0).astype(half)
    one = jnp.ones((), quarter)
    zero = jnp.zeros((), quarter)

    def hot(row_ref, row, size):
        values = jnp.broadcast_to(row_ref[pl.ds(row, 1), :], (32, depth)).astype(half)
        pieces = [jnp.where(values == rows_iota + 32 * k, one, zero) for k in range(size // 32)]
        return jnp.concatenate(pieces, 0)

    done = 0
    for level, (first, width, by_box) in enumerate(levels):
        pair = slice(2 * level, 2 * level + 2)
        for ref, rows in zip(lists[pair], scratch[pair]):
            if by_box:
                rows[...] = jnp.full(rows.shape, -1, jnp.float32)
                rows[:, : ref.shape[1]] = ref[first : first + width, :].astype(jnp.float32)
                continue
            length, total = ref.shape
            whole = length // 8 * 8
            begin = first // LANES * LANES
            span = min(rows.shape[0], total - begin)
            lanes = slice(begin, begin + span)
            pad = jnp.full((depth - length, span), -1, jnp.int32)
            entries = jnp.concatenate([ref[:whole, lanes], ref[whole:, lanes], pad], 0)
            rows[...] = entries.astype(jnp.float32).T
        source_rows, kind_rows = scratch[pair]
        offset = 0 if by_box else first % LANES

        def one_box(box, _):
            source_hot = hot(source_rows, box + offset, columns)
            kind_hot = hot(kind_rows, box + offset, kinds)
            counted = lax.dot_general(
                kind_hot, source_hot, (((1,), (1,)), ((), ())), preferred_element_type=jnp.float32
            )
            start = pl.multiple_of((box + done) * kinds, kinds)
            out_ref[pl.ds(start, kinds), :] = counted.astype(half)
            return 0

        lax.fori_loop(0, width, one_box, 0, unroll=min(width, 64))
        done += width


def count_entries(lists, length, levels, kinds, columns, after=()):
    depth = round_up(length, LANES)
    boxes = sum(width for _, width, _ in levels)
    scratch = []
    for first, width, by_box in levels:
        span = width if by_box else round_up(first % LANES + width, LANES)
        scratch += [pltpu.VMEM((span, depth), jnp.float32)] * 2
    return pl.pallas_call(
        functools.partial(count_kernel, levels, kinds, columns),
        out_shape=jax.ShapeDtypeStruct((boxes * kinds, columns), jnp.bfloat16),
        in_specs=[VMEM] * (len(lists) + len(after)),
        out_specs=VMEM,
        scratch_shapes=scratch,
        compiler_params=pltpu.CompilerParams(vmem_limit_bytes=8 << 20),
        cost_estimate=pl.CostEstimate(
            flops=2 * boxes * depth * kinds * columns * 4,
            bytes_accessed=boxes * kinds * columns * 2,
            transcendentals=0,
        ),
        name="counts",
    )(*lists, *after)


def local_kernel(widths, firsts, kinds, member_ref, *refs):
    counted, refs = refs[: len(firsts)], refs[len(firsts) :]
    (b0, b1, b2, b3, b4, ops_ref, coarse_ref, shift_ref, out_ref, grouped, total, moved) = refs
    blocks = (b0, b1, b2, b3, b4)
    member = member_ref[0]
    fine, parent = widths
    boxes = fine + parent
    coef = out_ref.shape[1]
    pitch = grouped.shape[0] // boxes

    for start in range(0, boxes, WINDOW):
        count = min(WINDOW, boxes - start)
        nearby = jnp.concatenate([ref[start : start + WINDOW, :] for ref in blocks], 0)
        which = max(i for i in range(len(firsts)) if firsts[i] <= start)
        at = (start - firsts[which]) * kinds
        values = jnp.dot(
            counted[which][at : at + count * kinds, :], nearby, preferred_element_type=jnp.float32
        )
        for box in range(count):
            row = (start + box) * pitch
            grouped[row : row + kinds, :] = values[box * kinds : (box + 1) * kinds]

    step = 8
    for at in range(0, kinds, step):
        picked = [
            grouped[pl.ds(at + k, boxes, stride=pitch), :].astype(jnp.bfloat16)
            for k in range(step)
        ]
        term = jnp.dot(
            jnp.concatenate(picked, 1),
            ops_ref[at * coef : (at + step) * coef, :],
            preferred_element_type=jnp.float32,
        )
        total[...] = term + total[...] if at else term
    begin = member * parent
    if parent % 8 == 0:
        begin = pl.multiple_of(begin, 8)
    parent_local = coarse_ref[pl.ds(begin, parent), :] + total[fine:, :]
    parent_local = parent_local.astype(jnp.bfloat16)
    octants = shift_ref.shape[0]
    for octant in range(octants):
        moved[pl.ds(octant, parent, stride=octants), :] = jnp.dot(
            parent_local, shift_ref[octant], preferred_element_type=jnp.float32
        )
    whole = moved[...] + total[:fine, :]
    keep = lax.broadcasted_iota(jnp.int32, whole.shape, 1) < NTERMS
    out_ref[...] = jnp.where(keep, whole, 0.0).astype(jnp.bfloat16)


def local_of(member, counted, firsts, blocks, flat_ops, coarse, child_shift, widths, kinds):
    fine, parent = widths
    coef = flat_ops.shape[1]
    boxes = fine + parent
    return pl.pallas_call(
        functools.partial(local_kernel, widths, firsts, kinds),
        out_shape=jax.ShapeDtypeStruct((fine, coef), jnp.bfloat16),
        in_specs=[SMEM] + [VMEM] * (8 + len(counted)),
        out_specs=VMEM,
        scratch_shapes=[
            pltpu.VMEM((boxes * (kinds + 4), coef), jnp.float32),
            pltpu.VMEM((boxes, coef), jnp.float32),
            pltpu.VMEM((fine, coef), jnp.float32),
        ],
        compiler_params=pltpu.CompilerParams(vmem_limit_bytes=24 << 20),
        cost_estimate=pl.CostEstimate(
            flops=8 * boxes * kinds * coef * 256,
            bytes_accessed=boxes * kinds * coef * 4,
            transcendentals=0,
        ),
        name="far",
    )(member, *counted, *blocks, flat_ops, coarse, child_shift)


def slots_of(basis_ref, counts_ref, box, local):
    count, coef = local.shape
    slots = basis_ref.shape[1]
    pairs = count // 2
    odd = lax.broadcasted_iota(jnp.int32, local.shape, 0) % 2
    zero = jnp.zeros_like(local)
    right = jnp.concatenate(
        [jnp.where(odd == 0, local, zero), jnp.where(odd == 1, local, zero)], 1
    )
    left = basis_ref[pl.ds(box, count)].reshape(pairs, 2, slots, coef)
    left = jnp.concatenate([left[:, 0], left[:, 1]], 2).reshape(pairs * slots, 2 * coef)
    values = lax.dot_general(
        left, right, (((1,), (1,)), ((), ())), preferred_element_type=jnp.float32
    ).reshape(pairs, slots, count)
    lane = lax.broadcasted_iota(jnp.int32, (slots, count), 1) // 2
    summed = jnp.zeros((slots, count), jnp.float32)
    for pair in range(pairs):
        summed += jnp.where(lane == pair, values[pair], 0.0)
    slot = lax.broadcasted_iota(jnp.int32, summed.shape, 0)
    limit = counts_ref[:, pl.ds(box, count)]
    return jnp.where(slot < limit, summed, 0.0)


def own_kernel(member_ref, local_ref, basis_ref, counts_ref, out_ref):
    width = local_ref.shape[0]
    for piece in range(width // LANES):
        box = pl.multiple_of(member_ref[0] * width + piece * LANES, LANES)
        at = slice(piece * LANES, (piece + 1) * LANES)
        out_ref[:, at] = slots_of(basis_ref, counts_ref, box, local_ref[at, :])


def other_kernel(member_ref, local_ref, basis_ref, counts_ref, own_ref, out_ref):
    width = local_ref.shape[0]
    out_ref[:, pl.ds(pl.multiple_of(member_ref[0] * width, LANES), width)] = own_ref[...]
    for piece in range(width // LANES):
        box = pl.multiple_of((1 - member_ref[0]) * width + piece * LANES, LANES)
        at = slice(piece * LANES, (piece + 1) * LANES)
        out_ref[:, pl.ds(box, LANES)] = slots_of(basis_ref, counts_ref, box, local_ref[at, :])


def evaluate(kernel, columns, member, local, basis, counts, *more):
    slots = basis.shape[1]
    return pl.pallas_call(
        kernel,
        out_shape=jax.ShapeDtypeStruct((slots, columns), jnp.float32),
        in_specs=[SMEM] + [VMEM] * (3 + len(more)),
        out_specs=VMEM,
        compiler_params=pltpu.CompilerParams(vmem_limit_bytes=16 << 20),
        cost_estimate=pl.CostEstimate(
            flops=2 * local.shape[0] * slots * 256 * 128,
            bytes_accessed=local.shape[0] * slots * 256,
            transcendentals=0,
        ),
        name="slots",
    )(member, local, basis, counts, *more)


def body(
    fine_parts,
    parent_parts,
    coarse_local,
    fine_source,
    fine_operator,
    parent_source,
    parent_operator,
    operators,
    child_shift,
    basis,
    counts,
):
    group = lax.axis_size("batch")
    member = lax.axis_index("batch")
    kinds, coef, _ = operators.shape
    fine_total, parent_total = fine_source.shape[1], parent_source.shape[1]
    widths = (fine_total // group, parent_total // group)
    index = member.astype(jnp.int32).reshape(1)

    lists = (fine_source, fine_operator, parent_source.T, parent_operator.T)
    special = group == 2 and widths[0] % (2 * LANES) == 0 and widths[1] % WINDOW == 0

    def share(whose):
        fine_size, parent_size = max(widths[0], WINDOW), max(widths[1], WINDOW)
        fine_at = whose * widths[0] // WINDOW * WINDOW
        parent_at = whose * widths[1] // WINDOW * WINDOW
        return jnp.concatenate(
            [
                lax.dynamic_slice_in_dim(fine_parts[0], fine_at, fine_size, 0),
                lax.dynamic_slice_in_dim(parent_parts[0], parent_at, parent_size, 0),
            ],
            0,
        )

    columns = 5 * WINDOW
    length = fine_source.shape[0]
    if special:
        mine, theirs, *lists = pack(index, fine_parts, parent_parts, lists, widths)
        early = widths[0] // 2
        late = widths[0] - early
        counted_late = ((early, late, False), (0, widths[1], True))
        summed = mine.astype(jnp.float32) + rotate(theirs, "batch", 1).astype(jnp.float32)
        own = summed.astype(jnp.bfloat16)
        counted = [
            count_entries(lists[:2], length, ((0, early, False),), kinds, columns),
            count_entries(lists, length, counted_late, kinds, columns, (own,)),
        ]
        firsts = (0, early)
    else:
        summed = share(member).astype(jnp.float32)
        for step in range(1, group):
            summed += rotate(share((member + step) % group), "batch", step).astype(jnp.float32)
        own = summed.astype(jnp.bfloat16)
        levels = ((0, widths[0], True), (0, widths[1], True))
        lists = [
            lax.dynamic_slice_in_dim(each, member * width, width, 0)
            for each, width in zip(
                (fine_source.T, fine_operator.T, *lists[2:]), (*widths[:1] * 2, *widths[1:] * 2)
            )
        ]
        counted = [count_entries(lists, length, levels, kinds, columns)]
        firsts = (0,)
    blocks = [own] + [partner(own, "space", bit) for bit in range(4)]
    local = local_of(
        index,
        counted,
        firsts,
        blocks,
        operators.reshape(kinds * coef, coef),
        coarse_local,
        child_shift,
        widths,
        kinds,
    )
    if special:
        other = rotate(local, "batch", 1)
        mine = evaluate(own_kernel, widths[0], index, local, basis, counts)
        return evaluate(other_kernel, fine_total, index, other, basis, counts, mine)
    gathered = jnp.zeros((fine_total, coef), local.dtype)
    for step in range(group):
        piece = rotate(local, "batch", step) if step else local
        at = (member - step) % group * widths[0]
        gathered = lax.dynamic_update_slice_in_dim(gathered, piece, at, 0)
    return evaluate(own_kernel, fine_total, index * 0, gathered, basis, counts)


def solution(mesh):
    placed = (
        P("batch", "space", None),
        P("batch", "space", None),
        P("space", None),
        P(None, "space"),
        P(None, "space"),
        P(None, "space"),
        P(None, "space"),
        P(),
        P(),
        P("space", "batch", None),
        P("batch", "space"),
    )
    return jax.shard_map(
        body, mesh=mesh, in_specs=placed, out_specs=P("batch", "space"), check_vma=False
    )
```

```python
import functools

import jax
import jax.numpy as jnp
from jax import lax
from jax.experimental import pallas as pl
from jax.experimental.pallas import tpu as pltpu
from jax.sharding import PartitionSpec as P


NTERMS = 121
WINDOW = 32
LANES = 128
VMEM = pl.BlockSpec(memory_space=pltpu.VMEM)
HBM = pl.BlockSpec(memory_space=pltpu.HBM)
SMEM = pl.BlockSpec(memory_space=pltpu.SMEM)


def round_up(value, step):
    return -(-value // step) * step


def rotate(value, axis, step):
    size = lax.axis_size(axis)
    return lax.ppermute(value, axis, [(i, (i + step) % size) for i in range(size)])


def partner(value, axis, apart):
    return lax.ppermute(value, axis, [(i, i ^ 1 << apart) for i in range(lax.axis_size(axis))])


def pack_kernel(widths, member_ref, fine_ref, parent_ref, mine_ref, theirs_ref, sem):
    member = member_ref[0]
    fine, parent = widths
    copies = []
    for at, out in ((1 - member, theirs_ref), (member, mine_ref)):
        for ref, width, row in ((fine_ref, fine, 0), (parent_ref, parent, fine)):
            start = pl.multiple_of(at * width, WINDOW)
            pair = ref.at[0, pl.ds(start, width), :], out.at[pl.ds(row, width), :]
            copies.append(pltpu.make_async_copy(*pair, sem.at[len(copies)]))
    for copy in copies:
        copy.start()
    for copy in copies:
        copy.wait()


def in_place(values):
    return [pltpu.with_memory_space_constraint(each, pltpu.HBM) for each in values]


def pack(member, fine_parts, parent_parts, widths):
    chunk = jax.ShapeDtypeStruct((sum(widths), fine_parts.shape[2]), fine_parts.dtype)
    return pl.pallas_call(
        functools.partial(pack_kernel, widths),
        out_shape=[chunk, chunk],
        in_specs=[SMEM, HBM, HBM],
        out_specs=[VMEM, VMEM],
        scratch_shapes=[pltpu.SemaphoreType.DMA((4,))],
        compiler_params=pltpu.CompilerParams(vmem_limit_bytes=4 << 20),
        name="pack",
    )(member, *in_place((fine_parts, parent_parts)))


def count_boxes(source_rows, kind_rows, first, width, kinds, columns, out_ref, done):
    depth = source_rows.shape[1]
    half, quarter = jnp.bfloat16, jnp.float8_e4m3fn
    rows_iota = lax.broadcasted_iota(jnp.int32, (32, depth), 0).astype(half)
    one = jnp.ones((), quarter)
    zero = jnp.zeros((), quarter)

    def hot(row_ref, row, size):
        values = jnp.broadcast_to(row_ref[pl.ds(row, 1), :], (32, depth)).astype(half)
        pieces = [jnp.where(values == rows_iota + 32 * k, one, zero) for k in range(size // 32)]
        return jnp.concatenate(pieces, 0)

    def one_box(box, _):
        source_hot = hot(source_rows, box + first, columns)
        kind_hot = hot(kind_rows, box + first, kinds)
        counted = lax.dot_general(
            kind_hot, source_hot, (((1,), (1,)), ((), ())), preferred_element_type=jnp.float32
        )
        start = pl.multiple_of((box + done) * kinds, kinds)
        out_ref[pl.ds(start, kinds), :] = counted.astype(half)
        return 0

    lax.fori_loop(0, width, one_box, 0, unroll=min(width, 64))


def first_kernel(early, kinds, columns, member_ref, *refs):
    lists, out_ref, rows, loaded, sem = refs[:4], refs[4], refs[5:9], refs[9:13], refs[13]
    member = member_ref[0]
    length, fine = loaded[0].shape
    parent = loaded[2].shape[0]
    lanes = pl.ds(pl.multiple_of(member * fine, LANES), fine)
    boxes = pl.ds(pl.multiple_of(member * parent, 8), parent)
    copies = [
        pltpu.make_async_copy(ref.at[where], out, sem.at[i])
        for i, (ref, where, out) in enumerate(
            zip(lists, ((slice(None), lanes),) * 2 + ((boxes, slice(None)),) * 2, loaded)
        )
    ]
    for copy in copies:
        copy.start()
    depth = rows[0].shape[1]
    whole = length // 8 * 8
    pad = jnp.full((depth - length, fine), -1, jnp.int32)
    for copy, ref, out in zip(copies[:2], loaded[:2], rows[:2]):
        copy.wait()
        entries = jnp.concatenate([ref[:whole, :], ref[whole:, :], pad], 0)
        out[...] = entries.astype(jnp.float32).T
    for copy, ref, out in zip(copies[2:], loaded[2:], rows[2:]):
        copy.wait()
        out[...] = jnp.full(out.shape, -1, jnp.float32)
        out[:, :length] = ref[...].astype(jnp.float32)
    count_boxes(*rows[:2], 0, early, kinds, columns, out_ref, 0)


def first_counts(member, lists, widths, early, kinds, columns):
    length = lists[0].shape[0]
    depth = round_up(length, LANES)
    rows = [jax.ShapeDtypeStruct((width, depth), jnp.float32) for width in widths for _ in "ab"]
    loaded = [pltpu.VMEM((length, widths[0]), jnp.int32)] * 2
    loaded += [pltpu.VMEM((widths[1], length), jnp.int32)] * 2
    return pl.pallas_call(
        functools.partial(first_kernel, early, kinds, columns),
        out_shape=[jax.ShapeDtypeStruct((early * kinds, columns), jnp.bfloat16)] + rows,
        in_specs=[SMEM] + [HBM] * 4,
        out_specs=[VMEM] * 5,
        scratch_shapes=loaded + [pltpu.SemaphoreType.DMA((4,))],
        compiler_params=pltpu.CompilerParams(vmem_limit_bytes=8 << 20),
        cost_estimate=count_cost(early, depth, kinds, columns),
        name="first_counts",
    )(member, *in_place(lists))


def count_cost(boxes, depth, kinds, columns):
    return pl.CostEstimate(
        flops=8 * boxes * depth * kinds * columns,
        bytes_accessed=boxes * kinds * columns * 2,
        transcendentals=0,
    )


def count_kernel(levels, kinds, columns, *refs):
    out_ref = refs[-1]
    done = 0
    for level, (first, width) in enumerate(levels):
        rows = refs[2 * level : 2 * level + 2]
        count_boxes(*rows, first, width, kinds, columns, out_ref, done)
        done += width


def count_entries(rows, levels, kinds, columns, after=()):
    boxes = sum(width for _, width in levels)
    return pl.pallas_call(
        functools.partial(count_kernel, levels, kinds, columns),
        out_shape=jax.ShapeDtypeStruct((boxes * kinds, columns), jnp.bfloat16),
        in_specs=[VMEM] * (len(rows) + len(after)),
        out_specs=VMEM,
        compiler_params=pltpu.CompilerParams(vmem_limit_bytes=8 << 20),
        cost_estimate=count_cost(boxes, rows[0].shape[1], kinds, columns),
        name="counts",
    )(*rows, *after)


def local_kernel(widths, firsts, kinds, member_ref, *refs):
    counted, refs = refs[: len(firsts)], refs[len(firsts) :]
    (b0, b1, b2, b3, b4, ops_ref, coarse_ref, shift_ref, out_ref, grouped, total, moved) = refs
    blocks = (b0, b1, b2, b3, b4)
    member = member_ref[0]
    fine, parent = widths
    boxes = fine + parent
    coef = out_ref.shape[1]
    pitch = grouped.shape[0] // boxes

    for start in range(0, boxes, WINDOW):
        count = min(WINDOW, boxes - start)
        nearby = jnp.concatenate([ref[start : start + WINDOW, :] for ref in blocks], 0)
        which = max(i for i in range(len(firsts)) if firsts[i] <= start)
        at = (start - firsts[which]) * kinds
        values = jnp.dot(
            counted[which][at : at + count * kinds, :], nearby, preferred_element_type=jnp.float32
        )
        for box in range(count):
            row = (start + box) * pitch
            grouped[row : row + kinds, :] = values[box * kinds : (box + 1) * kinds]

    step = 8
    for at in range(0, kinds, step):
        picked = [
            grouped[pl.ds(at + k, boxes, stride=pitch), :].astype(jnp.bfloat16)
            for k in range(step)
        ]
        term = jnp.dot(
            jnp.concatenate(picked, 1),
            ops_ref[at * coef : (at + step) * coef, :],
            preferred_element_type=jnp.float32,
        )
        total[...] = term + total[...] if at else term
    begin = member * parent
    if parent % 8 == 0:
        begin = pl.multiple_of(begin, 8)
    parent_local = coarse_ref[pl.ds(begin, parent), :] + total[fine:, :]
    parent_local = parent_local.astype(jnp.bfloat16)
    octants = shift_ref.shape[0]
    for octant in range(octants):
        moved[pl.ds(octant, parent, stride=octants), :] = jnp.dot(
            parent_local, shift_ref[octant], preferred_element_type=jnp.float32
        )
    whole = moved[...] + total[:fine, :]
    keep = lax.broadcasted_iota(jnp.int32, whole.shape, 1) < NTERMS
    out_ref[...] = jnp.where(keep, whole, 0.0).astype(jnp.bfloat16)


def local_of(member, counted, firsts, blocks, flat_ops, coarse, child_shift, widths, kinds):
    fine, parent = widths
    coef = flat_ops.shape[1]
    boxes = fine + parent
    return pl.pallas_call(
        functools.partial(local_kernel, widths, firsts, kinds),
        out_shape=jax.ShapeDtypeStruct((fine, coef), jnp.bfloat16),
        in_specs=[SMEM] + [VMEM] * (8 + len(counted)),
        out_specs=VMEM,
        scratch_shapes=[
            pltpu.VMEM((boxes * (kinds + 4), coef), jnp.float32),
            pltpu.VMEM((boxes, coef), jnp.float32),
            pltpu.VMEM((fine, coef), jnp.float32),
        ],
        compiler_params=pltpu.CompilerParams(vmem_limit_bytes=24 << 20),
        cost_estimate=pl.CostEstimate(
            flops=8 * boxes * kinds * coef * 256,
            bytes_accessed=boxes * kinds * coef * 4,
            transcendentals=0,
        ),
        name="far",
    )(member, *counted, *blocks, flat_ops, coarse, child_shift)


def slots_of(basis_ref, counts_ref, box, local):
    count, coef = local.shape
    slots = basis_ref.shape[1]
    pairs = count // 2
    odd = lax.broadcasted_iota(jnp.int32, local.shape, 0) % 2
    zero = jnp.zeros_like(local)
    right = jnp.concatenate(
        [jnp.where(odd == 0, local, zero), jnp.where(odd == 1, local, zero)], 1
    )
    left = basis_ref[pl.ds(box, count)].reshape(pairs, 2, slots, coef)
    left = jnp.concatenate([left[:, 0], left[:, 1]], 2).reshape(pairs * slots, 2 * coef)
    values = lax.dot_general(
        left, right, (((1,), (1,)), ((), ())), preferred_element_type=jnp.float32
    ).reshape(pairs, slots, count)
    lane = lax.broadcasted_iota(jnp.int32, (slots, count), 1) // 2
    summed = jnp.zeros((slots, count), jnp.float32)
    for pair in range(pairs):
        summed += jnp.where(lane == pair, values[pair], 0.0)
    slot = lax.broadcasted_iota(jnp.int32, summed.shape, 0)
    limit = counts_ref[:, pl.ds(box, count)]
    return jnp.where(slot < limit, summed, 0.0)


def own_kernel(member_ref, local_ref, basis_ref, counts_ref, out_ref):
    width = local_ref.shape[0]
    for piece in range(width // LANES):
        box = pl.multiple_of(member_ref[0] * width + piece * LANES, LANES)
        at = slice(piece * LANES, (piece + 1) * LANES)
        out_ref[:, at] = slots_of(basis_ref, counts_ref, box, local_ref[at, :])


def other_kernel(member_ref, local_ref, basis_ref, counts_ref, own_ref, out_ref):
    width = local_ref.shape[0]
    out_ref[:, pl.ds(pl.multiple_of(member_ref[0] * width, LANES), width)] = own_ref[...]
    for piece in range(width // LANES):
        box = pl.multiple_of((1 - member_ref[0]) * width + piece * LANES, LANES)
        at = slice(piece * LANES, (piece + 1) * LANES)
        out_ref[:, pl.ds(box, LANES)] = slots_of(basis_ref, counts_ref, box, local_ref[at, :])


def evaluate(kernel, columns, member, local, basis, counts, *more):
    slots = basis.shape[1]
    return pl.pallas_call(
        kernel,
        out_shape=jax.ShapeDtypeStruct((slots, columns), jnp.float32),
        in_specs=[SMEM] + [VMEM] * (3 + len(more)),
        out_specs=VMEM,
        compiler_params=pltpu.CompilerParams(vmem_limit_bytes=16 << 20),
        cost_estimate=pl.CostEstimate(
            flops=2 * local.shape[0] * slots * 256 * 128,
            bytes_accessed=local.shape[0] * slots * 256,
            transcendentals=0,
        ),
        name="slots",
    )(member, local, basis, counts, *more)


def body(
    fine_parts,
    parent_parts,
    coarse_local,
    fine_source,
    fine_operator,
    parent_source,
    parent_operator,
    operators,
    child_shift,
    basis,
    counts,
):
    group = lax.axis_size("batch")
    member = lax.axis_index("batch")
    kinds, coef, _ = operators.shape
    fine_total, parent_total = fine_source.shape[1], parent_source.shape[1]
    widths = (fine_total // group, parent_total // group)
    index = member.astype(jnp.int32).reshape(1)

    lists = (fine_source, fine_operator, parent_source.T, parent_operator.T)
    special = group == 2 and widths[0] % (8 * WINDOW) == 0 and widths[1] % WINDOW == 0

    def share(whose):
        fine_size, parent_size = max(widths[0], WINDOW), max(widths[1], WINDOW)
        fine_at = whose * widths[0] // WINDOW * WINDOW
        parent_at = whose * widths[1] // WINDOW * WINDOW
        return jnp.concatenate(
            [
                lax.dynamic_slice_in_dim(fine_parts[0], fine_at, fine_size, 0),
                lax.dynamic_slice_in_dim(parent_parts[0], parent_at, parent_size, 0),
            ],
            0,
        )

    columns = 5 * WINDOW
    length = fine_source.shape[0]
    if special:
        mine, theirs = pack(index, fine_parts, parent_parts, widths)
        early = widths[0] // 2
        late = widths[0] - early
        firsts = (0, early)
        summed = mine.astype(jnp.float32) + rotate(theirs, "batch", 1).astype(jnp.float32)
        own = summed.astype(jnp.bfloat16)
        counted, *rows = first_counts(index, lists, widths, early, kinds, columns)
        levels = ((early, late), (0, widths[1]))
        counted = [counted, count_entries(rows, levels, kinds, columns, (own,))]
    else:
        summed = share(member).astype(jnp.float32)
        for step in range(1, group):
            summed += rotate(share((member + step) % group), "batch", step).astype(jnp.float32)
        own = summed.astype(jnp.bfloat16)
        depth = round_up(length, LANES)
        rows = []
        for each, width in zip(
            (fine_source.T, fine_operator.T, *lists[2:]), (*widths[:1] * 2, *widths[1:] * 2)
        ):
            each = lax.dynamic_slice_in_dim(each, member * width, width, 0).astype(jnp.float32)
            rows.append(jnp.pad(each, ((0, 0), (0, depth - length)), constant_values=-1))
        levels = ((0, widths[0]), (0, widths[1]))
        counted = [count_entries(rows, levels, kinds, columns)]
        firsts = (0,)
    blocks = [own]
    for bit in range(4):
        blocks.append(partner(own, "space", bit))
    local = local_of(
        index,
        counted,
        firsts,
        blocks,
        operators.reshape(kinds * coef, coef),
        coarse_local,
        child_shift,
        widths,
        kinds,
    )
    if special:
        other = rotate(local, "batch", 1)
        mine = evaluate(own_kernel, widths[0], index, local, basis, counts)
        return evaluate(other_kernel, fine_total, index, other, basis, counts, mine)
    gathered = jnp.zeros((fine_total, coef), local.dtype)
    for step in range(group):
        piece = rotate(local, "batch", step) if step else local
        at = (member - step) % group * widths[0]
        gathered = lax.dynamic_update_slice_in_dim(gathered, piece, at, 0)
    return evaluate(own_kernel, fine_total, index * 0, gathered, basis, counts)


def solution(mesh):
    placed = (
        P("batch", "space", None),
        P("batch", "space", None),
        P("space", None),
        P(None, "space"),
        P(None, "space"),
        P(None, "space"),
        P(None, "space"),
        P(),
        P(),
        P("space", "batch", None),
        P("batch", "space"),
    )

    return jax.shard_map(
        body, mesh=mesh, in_specs=placed, out_specs=P("batch", "space"), check_vma=False
    )
```

```python
import functools

import jax
import jax.numpy as jnp
from jax import lax
from jax.experimental import pallas as pl
from jax.experimental.pallas import tpu as pltpu
from jax.sharding import PartitionSpec as P


NTERMS = 121
WINDOW = 32
LANES = 128
VMEM = pl.BlockSpec(memory_space=pltpu.VMEM)
HBM = pl.BlockSpec(memory_space=pltpu.HBM)
SMEM = pl.BlockSpec(memory_space=pltpu.SMEM)


def round_up(value, step):
    return -(-value // step) * step


def rotate(value, axis, step):
    size = lax.axis_size(axis)
    return lax.ppermute(value, axis, [(i, (i + step) % size) for i in range(size)])


def partner(value, axis, apart):
    return lax.ppermute(value, axis, [(i, i ^ 1 << apart) for i in range(lax.axis_size(axis))])


def pack_kernel(widths, member_ref, fine_ref, parent_ref, mine_ref, theirs_ref, sem):
    member = member_ref[0]
    fine, parent = widths
    copies = []
    for at, out in ((1 - member, theirs_ref), (member, mine_ref)):
        start = pl.multiple_of(at * fine, WINDOW)
        for source, row, width in (
            (fine_ref.at[0, pl.ds(start, fine), :], 0, fine),
            (parent_ref.at[0], fine, parent),
        ):
            target = out.at[pl.ds(row, width), :]
            copies.append(pltpu.make_async_copy(source, target, sem.at[len(copies)]))
    for copy in copies:
        copy.start()
    for copy in copies:
        copy.wait()


def in_place(values):
    return [pltpu.with_memory_space_constraint(each, pltpu.HBM) for each in values]


def pack(member, fine_parts, parent_parts, widths):
    chunk = jax.ShapeDtypeStruct((sum(widths), fine_parts.shape[2]), fine_parts.dtype)
    return pl.pallas_call(
        functools.partial(pack_kernel, widths),
        out_shape=[chunk, chunk],
        in_specs=[SMEM, HBM, HBM],
        out_specs=[VMEM, VMEM],
        scratch_shapes=[pltpu.SemaphoreType.DMA((4,))],
        compiler_params=pltpu.CompilerParams(vmem_limit_bytes=4 << 20),
        name="pack",
    )(member, *in_place((fine_parts, parent_parts)))


def count_boxes(source_rows, kind_rows, first, width, kinds, columns, out_ref):
    depth = source_rows.shape[1]
    half, quarter = jnp.bfloat16, jnp.float8_e4m3fn
    rows_iota = lax.broadcasted_iota(jnp.int32, (32, depth), 0).astype(half)
    one = jnp.ones((), quarter)
    zero = jnp.zeros((), quarter)

    def hot(row_ref, row, size):
        values = jnp.broadcast_to(row_ref[pl.ds(row, 1), :], (32, depth)).astype(half)
        pieces = [jnp.where(values == rows_iota + 32 * k, one, zero) for k in range(size // 32)]
        return jnp.concatenate(pieces, 0)

    def one_box(box, _):
        source_hot = hot(source_rows, box + first, columns)
        kind_hot = hot(kind_rows, box + first, kinds)
        counted = lax.dot_general(
            kind_hot, source_hot, (((1,), (1,)), ((), ())), preferred_element_type=jnp.float32
        )
        start = pl.multiple_of(box * kinds, kinds)
        out_ref[pl.ds(start, kinds), :] = counted.astype(half)
        return 0

    lax.fori_loop(0, width, one_box, 0, unroll=min(width, 64))


def first_kernel(early, kinds, columns, member_ref, *refs):
    lists, out_ref, rows, loaded, sem = refs[:4], refs[4], refs[5:9], refs[9:13], refs[13]
    member = member_ref[0]
    length, fine = loaded[0].shape
    lanes = pl.ds(pl.multiple_of(member * fine, LANES), fine)
    sources = [ref.at[:, lanes] for ref in lists[:2]] + list(lists[2:])
    copies = [
        pltpu.make_async_copy(ref, out, sem.at[i]) for i, (ref, out) in enumerate(zip(sources, loaded))
    ]
    for copy in copies:
        copy.start()
    depth = rows[0].shape[1]
    whole = length // 8 * 8
    pad = jnp.full((depth - length, fine), -1, jnp.int32)
    for copy, ref, out in zip(copies[:2], loaded[:2], rows[:2]):
        copy.wait()
        entries = jnp.concatenate([ref[:whole, :], ref[whole:, :], pad], 0)
        out[...] = entries.astype(jnp.float32).T
    for copy, ref, out in zip(copies[2:], loaded[2:], rows[2:]):
        copy.wait()
        out[...] = jnp.full(out.shape, -1, jnp.float32)
        out[:, :length] = ref[...].astype(jnp.float32)
    count_boxes(*rows[:2], 0, early, kinds, columns, out_ref)


def first_counts(member, lists, widths, early, kinds, columns):
    length = lists[0].shape[0]
    depth = round_up(length, LANES)
    rows = [jax.ShapeDtypeStruct((width, depth), jnp.float32) for width in widths for _ in "ab"]
    loaded = [pltpu.VMEM((length, widths[0]), jnp.int32)] * 2
    loaded += [pltpu.VMEM((widths[1], length), jnp.int32)] * 2
    return pl.pallas_call(
        functools.partial(first_kernel, early, kinds, columns),
        out_shape=[jax.ShapeDtypeStruct((early * kinds, columns), jnp.bfloat16)] + rows,
        in_specs=[SMEM] + [HBM] * 4,
        out_specs=[VMEM] * 5,
        scratch_shapes=loaded + [pltpu.SemaphoreType.DMA((4,))],
        compiler_params=pltpu.CompilerParams(vmem_limit_bytes=8 << 20),
        cost_estimate=count_cost(early, depth, kinds, columns),
        name="first_counts",
    )(member, *in_place(lists))


def count_cost(boxes, depth, kinds, columns):
    return pl.CostEstimate(
        flops=8 * boxes * depth * kinds * columns,
        bytes_accessed=boxes * kinds * columns * 2,
        transcendentals=0,
    )


def count_kernel(levels, kinds, columns, *refs):
    for level, (first, width) in enumerate(levels):
        rows = refs[2 * level : 2 * level + 2]
        out_ref = refs[level - len(levels)]
        count_boxes(*rows, first, width, kinds, columns, out_ref)


def count_entries(rows, levels, kinds, columns, after=()):
    boxes = [width for _, width in levels]
    return pl.pallas_call(
        functools.partial(count_kernel, levels, kinds, columns),
        out_shape=[jax.ShapeDtypeStruct((each * kinds, columns), jnp.bfloat16) for each in boxes],
        in_specs=[VMEM] * (len(rows) + len(after)),
        out_specs=[VMEM] * len(boxes),
        compiler_params=pltpu.CompilerParams(vmem_limit_bytes=8 << 20),
        cost_estimate=count_cost(sum(boxes), rows[0].shape[1], kinds, columns),
        name="counts",
    )(*rows, *after)


def contract(counted, firsts, blocks, begin, kinds, ops_ref, grouped, total):
    boxes, coef = total.shape
    pitch = grouped.shape[0] // boxes
    for start in range(0, boxes, WINDOW):
        count = min(WINDOW, boxes - start)
        at = begin + start
        nearby = jnp.concatenate([ref[at : at + WINDOW, :] for ref in blocks], 0)
        which = max(i for i in range(len(firsts)) if firsts[i] <= start)
        at = (start - firsts[which]) * kinds
        values = jnp.dot(
            counted[which][at : at + count * kinds, :], nearby, preferred_element_type=jnp.float32
        )
        for box in range(count):
            row = (start + box) * pitch
            grouped[row : row + kinds, :] = values[box * kinds : (box + 1) * kinds]

    step = 8
    for at in range(0, kinds, step):
        picked = [
            grouped[pl.ds(at + k, boxes, stride=pitch), :].astype(jnp.bfloat16)
            for k in range(step)
        ]
        term = jnp.dot(
            jnp.concatenate(picked, 1),
            ops_ref[at * coef : (at + step) * coef, :],
            preferred_element_type=jnp.float32,
        )
        total[...] = term + total[...] if at else term


def contract_scratch(boxes, kinds, coef):
    return [pltpu.VMEM((boxes * (kinds + 4), coef), jnp.float32), pltpu.VMEM((boxes, coef), jnp.float32)]


def far_kernel(firsts, kinds, *refs):
    counted, blocks = refs[: len(firsts)], refs[len(firsts) : len(firsts) + 5]
    ops_ref, out_ref, grouped, total = refs[len(firsts) + 5 :]
    contract(counted, firsts, blocks, 0, kinds, ops_ref, grouped, total)
    out_ref[...] = total[...].astype(out_ref.dtype)


def far_of(counted, firsts, blocks, flat_ops, boxes, kinds):
    coef = flat_ops.shape[1]
    return pl.pallas_call(
        functools.partial(far_kernel, firsts, kinds),
        out_shape=jax.ShapeDtypeStruct((boxes, coef), jnp.bfloat16),
        in_specs=[VMEM] * (6 + len(counted)),
        out_specs=VMEM,
        scratch_shapes=contract_scratch(boxes, kinds, coef),
        compiler_params=pltpu.CompilerParams(vmem_limit_bytes=24 << 20),
        cost_estimate=pl.CostEstimate(
            flops=8 * boxes * kinds * coef * 256,
            bytes_accessed=boxes * kinds * coef * 4,
            transcendentals=0,
        ),
        name="far",
    )(*counted, *blocks, flat_ops)


def slots_of(basis_ref, counts_ref, box, local):
    count, coef = local.shape
    slots = basis_ref.shape[1]
    pairs = count // 2
    odd = lax.broadcasted_iota(jnp.int32, local.shape, 0) % 2
    zero = jnp.zeros_like(local)
    right = jnp.concatenate(
        [jnp.where(odd == 0, local, zero), jnp.where(odd == 1, local, zero)], 1
    )
    left = basis_ref[pl.ds(box, count)].reshape(pairs, 2, slots, coef)
    left = jnp.concatenate([left[:, 0], left[:, 1]], 2).reshape(pairs * slots, 2 * coef)
    values = lax.dot_general(
        left, right, (((1,), (1,)), ((), ())), preferred_element_type=jnp.float32
    ).reshape(pairs, slots, count)
    lane = lax.broadcasted_iota(jnp.int32, (slots, count), 1) // 2
    summed = jnp.zeros((slots, count), jnp.float32)
    for pair in range(pairs):
        summed += jnp.where(lane == pair, values[pair], 0.0)
    slot = lax.broadcasted_iota(jnp.int32, summed.shape, 0)
    limit = counts_ref[:, pl.ds(box, count)]
    return jnp.where(slot < limit, summed, 0.0)


def evaluate(far, moved, basis_ref, counts_ref, first):
    whole = moved + far.astype(jnp.float32)
    keep = lax.broadcasted_iota(jnp.int32, whole.shape, 1) < NTERMS
    local = jnp.where(keep, whole, 0.0).astype(jnp.bfloat16)
    width = local.shape[0]
    pieces = []
    for piece in range(0, width, LANES):
        box = pl.multiple_of(first + piece, LANES)
        pieces.append(slots_of(basis_ref, counts_ref, box, local[piece : piece + LANES]))
    return jnp.concatenate(pieces, 1)


def own_kernel(kinds, fine, member_ref, count_ref, *refs):
    blocks = refs[:5]
    (ops_ref, coarse_ref, shift_ref, far_ref, basis_ref, counts_ref) = refs[5:11]
    out_ref, rest_ref, grouped, total, moved = refs[11:]
    contract((count_ref,), (0,), blocks, fine, kinds, ops_ref, grouped, total)
    parent_local = (coarse_ref[...] + total[...]).astype(jnp.bfloat16)
    parents = parent_local.shape[0]
    octants = shift_ref.shape[0]
    for octant in range(octants):
        moved[pl.ds(octant, parents, stride=octants), :] = jnp.dot(
            parent_local, shift_ref[octant], preferred_element_type=jnp.float32
        )
    width = far_ref.shape[0]
    first = pl.multiple_of(member_ref[0] * width, LANES)
    out_ref[...] = evaluate(
        far_ref[...], moved[pl.ds(first, width), :], basis_ref, counts_ref, first
    )
    rest = rest_ref.shape[0]
    rest_ref[...] = moved[pl.ds(pl.multiple_of((1 - member_ref[0]) * rest, LANES), rest), :]


def own_of(member, counted, blocks, fine, flat_ops, coarse, shift, far, basis, counts, kinds, rest):
    slots, coef = basis.shape[1:]
    parents = coarse.shape[0]
    return pl.pallas_call(
        functools.partial(own_kernel, kinds, fine),
        out_shape=[
            jax.ShapeDtypeStruct((slots, far.shape[0]), jnp.float32),
            jax.ShapeDtypeStruct((rest, coef), jnp.float32),
        ],
        in_specs=[SMEM] + [VMEM] * 12,
        out_specs=[VMEM, VMEM],
        scratch_shapes=contract_scratch(parents, kinds, coef)
        + [pltpu.VMEM((parents * shift.shape[0], coef), jnp.float32)],
        compiler_params=pltpu.CompilerParams(vmem_limit_bytes=16 << 20),
        cost_estimate=pl.CostEstimate(
            flops=8 * parents * kinds * coef * 256,
            bytes_accessed=parents * kinds * coef * 4,
            transcendentals=0,
        ),
        name="own",
    )(member, counted, *blocks, flat_ops, coarse, shift, far, basis, counts)


def other_kernel(member_ref, far_ref, moved_ref, basis_ref, counts_ref, own_ref, out_ref):
    width = far_ref.shape[0]
    out_ref[:, pl.ds(pl.multiple_of(member_ref[0] * width, LANES), width)] = own_ref[...]
    first = pl.multiple_of((1 - member_ref[0]) * width, LANES)
    out_ref[:, pl.ds(first, width)] = evaluate(
        far_ref[...], moved_ref[...], basis_ref, counts_ref, first
    )


def other_of(member, far, moved, basis, counts, own):
    slots = basis.shape[1]
    return pl.pallas_call(
        other_kernel,
        out_shape=jax.ShapeDtypeStruct((slots, basis.shape[0]), jnp.float32),
        in_specs=[SMEM] + [VMEM] * 5,
        out_specs=VMEM,
        compiler_params=pltpu.CompilerParams(vmem_limit_bytes=16 << 20),
        cost_estimate=pl.CostEstimate(
            flops=2 * far.shape[0] * slots * 256 * 128,
            bytes_accessed=far.shape[0] * slots * 256,
            transcendentals=0,
        ),
        name="other",
    )(member, far, moved, basis, counts, own)


def body(
    fine_parts,
    parent_parts,
    coarse_local,
    fine_source,
    fine_operator,
    parent_source,
    parent_operator,
    operators,
    child_shift,
    basis,
    counts,
):
    group = lax.axis_size("batch")
    member = lax.axis_index("batch")
    kinds, coef, _ = operators.shape
    fine_total, parent_total = fine_source.shape[1], parent_source.shape[1]
    fine = fine_total // group
    widths = (fine, parent_total)
    index = member.astype(jnp.int32).reshape(1)
    lists = (fine_source, fine_operator, parent_source.T, parent_operator.T)
    special = group == 2 and fine % (8 * WINDOW) == 0

    def share(whose):
        fine_at = whose * fine // WINDOW * WINDOW
        mine = lax.dynamic_slice_in_dim(fine_parts[0], fine_at, max(fine, WINDOW), 0)
        return jnp.concatenate([mine, parent_parts[0]], 0)

    columns = 5 * WINDOW
    length = fine_source.shape[0]
    if special:
        mine, theirs = pack(index, fine_parts, parent_parts, widths)
        early = fine // 2
        summed = mine.astype(jnp.float32) + rotate(theirs, "batch", 1).astype(jnp.float32)
        own = summed.astype(jnp.bfloat16)
        counted, *rows = first_counts(index, lists, widths, early, kinds, columns)
        levels = ((early, fine - early), (0, parent_total))
        late, parent_counted = count_entries(rows, levels, kinds, columns, (own,))
        counted = [counted, late]
        firsts = (0, early)
    else:
        summed = share(member).astype(jnp.float32)
        for step in range(1, group):
            summed += rotate(share((member + step) % group), "batch", step).astype(jnp.float32)
        own = summed.astype(jnp.bfloat16)
        fine_lists = [
            lax.dynamic_slice_in_dim(each.T, member * fine, fine, 0) for each in lists[:2]
        ]
        rows = [
            jnp.pad(
                each.astype(jnp.float32),
                ((0, 0), (0, round_up(length, LANES) - length)),
                constant_values=-1,
            )
            for each in (*fine_lists, *lists[2:])
        ]
        *counted, parent_counted = count_entries(
            rows, ((0, fine), (0, parent_total)), kinds, columns
        )
        firsts = (0,)
    blocks = [own]
    for bit in range(4):
        blocks.append(partner(own, "space", bit))
    flat_ops = operators.reshape(kinds * coef, coef)
    far = far_of(counted, firsts, blocks, flat_ops, fine, kinds)
    fine_rows = max(fine, WINDOW)
    parent_side = (parent_counted, blocks, fine_rows, flat_ops, coarse_local, child_shift)
    if special:
        other = rotate(far, "batch", 1)
        mine, moved = own_of(index, *parent_side, far, basis, counts, kinds, fine)
        return other_of(index, other, moved, basis, counts, mine)
    gathered = jnp.zeros((fine_total, coef), far.dtype)
    for step in range(group):
        piece = rotate(far, "batch", step) if step else far
        at = (member - step) % group * fine
        gathered = lax.dynamic_update_slice_in_dim(gathered, piece, at, 0)
    values, _ = own_of(index * 0, *parent_side, gathered, basis, counts, kinds, LANES)
    return values


def solution(mesh):
    placed = (
        P("batch", "space", None),
        P("batch", "space", None),
        P("space", None),
        P(None, "space"),
        P(None, "space"),
        P(None, "space"),
        P(None, "space"),
        P(),
        P(),
        P("space", "batch", None),
        P("batch", "space"),
    )

    return jax.shard_map(
        body, mesh=mesh, in_specs=placed, out_specs=P("batch", "space"), check_vma=False
    )
```

```python
import functools

import jax
import jax.numpy as jnp
from jax import lax
from jax.experimental import pallas as pl
from jax.experimental.pallas import tpu as pltpu
from jax.sharding import PartitionSpec as P


NTERMS = 121
WINDOW = 32
LANES = 128
HOPS = ((2, 3, 1, 0), (3, 2, 1, 0))
VMEM = pl.BlockSpec(memory_space=pltpu.VMEM)
HBM = pl.BlockSpec(memory_space=pltpu.HBM)
SMEM = pl.BlockSpec(memory_space=pltpu.SMEM)


def round_up(value, step):
    return -(-value // step) * step


def rotate(value, axis, step):
    size = lax.axis_size(axis)
    return lax.ppermute(value, axis, [(i, (i + step) % size) for i in range(size)])


def colour(index):
    bits = index >> 1
    for shift in (8, 4, 2, 1):
        bits = bits ^ bits >> shift
    return bits & 1


def hop_to_partner(value, axis, hop):
    apart = [order[hop] for order in HOPS]
    pairs = [(i, i ^ 1 << apart[colour(i)]) for i in range(lax.axis_size(axis))]
    return lax.ppermute(value, axis, pairs)


def pack_kernel(widths, member_ref, tint_ref, fine_ref, parent_ref, mine_ref, theirs_ref, sem):
    member = member_ref[0]
    fine, parent = widths
    copies = []
    for at, out in ((1 - member, theirs_ref), (member, mine_ref)):
        start = pl.multiple_of(at * fine, WINDOW)
        for source, row, width in (
            (fine_ref.at[0, pl.ds(start, fine), :], 0, fine),
            (parent_ref.at[0], fine, parent),
        ):
            target = out.at[pl.ds(row, width), :]
            copies.append(pltpu.make_async_copy(source, target, sem.at[len(copies)]))
    for copy in copies:
        copy.start()
    for copy in copies:
        copy.wait()


def in_place(values):
    return [pltpu.with_memory_space_constraint(each, pltpu.HBM) for each in values]


def pack(member, tint, fine_parts, parent_parts, widths):
    chunk = jax.ShapeDtypeStruct((sum(widths), fine_parts.shape[2]), fine_parts.dtype)
    return pl.pallas_call(
        functools.partial(pack_kernel, widths),
        out_shape=[chunk, chunk],
        in_specs=[SMEM, SMEM, HBM, HBM],
        out_specs=[VMEM, VMEM],
        scratch_shapes=[pltpu.SemaphoreType.DMA((4,))],
        compiler_params=pltpu.CompilerParams(vmem_limit_bytes=4 << 20),
        name="pack",
    )(member, tint, *in_place((fine_parts, parent_parts)))


def count_boxes(source_rows, kind_rows, first, width, kinds, columns, out_ref):
    depth = source_rows.shape[1]
    half, quarter = jnp.bfloat16, jnp.float8_e4m3fn
    rows_iota = lax.broadcasted_iota(jnp.int32, (32, depth), 0).astype(half)
    one = jnp.ones((), quarter)
    zero = jnp.zeros((), quarter)

    def hot(row_ref, row, size):
        values = jnp.broadcast_to(row_ref[pl.ds(row, 1), :], (32, depth)).astype(half)
        pieces = [jnp.where(values == rows_iota + 32 * k, one, zero) for k in range(size // 32)]
        return jnp.concatenate(pieces, 0)

    def one_box(box, _):
        source_hot = hot(source_rows, box + first, columns)
        kind_hot = hot(kind_rows, box + first, kinds)
        counted = lax.dot_general(
            kind_hot, source_hot, (((1,), (1,)), ((), ())), preferred_element_type=jnp.float32
        )
        start = pl.multiple_of((box + first) * kinds, kinds)
        out_ref[pl.ds(start, kinds), :] = counted.astype(half)
        return 0

    lax.fori_loop(0, width, one_box, 0, unroll=min(width, 128))


def first_kernel(early, kinds, columns, member_ref, *refs):
    lists, out_ref, rows, loaded, sem = refs[:4], refs[4], refs[5:9], refs[9:13], refs[13]
    member = member_ref[0]
    length, fine = loaded[0].shape
    lanes = pl.ds(pl.multiple_of(member * fine, LANES), fine)
    sources = [ref.at[:, lanes] for ref in lists[:2]] + list(lists[2:])
    copies = [
        pltpu.make_async_copy(ref, out, sem.at[i]) for i, (ref, out) in enumerate(zip(sources, loaded))
    ]
    for copy in copies:
        copy.start()
    depth = rows[0].shape[1]
    whole = length // 8 * 8
    pad = jnp.full((depth - length, fine), -1, jnp.int32)
    for copy, ref, out in zip(copies[:2], loaded[:2], rows[:2]):
        copy.wait()
        entries = jnp.concatenate([ref[:whole, :], ref[whole:, :], pad], 0)
        out[...] = entries.astype(jnp.float32).T
    for copy, ref, out in zip(copies[2:], loaded[2:], rows[2:]):
        copy.wait()
        out[...] = jnp.full(out.shape, -1, jnp.float32)
        out[:, :length] = ref[...].astype(jnp.float32)
    count_boxes(*rows[:2], 0, early, kinds, columns, out_ref)


def first_counts(member, lists, widths, early, kinds, columns):
    length = lists[0].shape[0]
    depth = round_up(length, LANES)
    rows = [jax.ShapeDtypeStruct((width, depth), jnp.float32) for width in widths for _ in "ab"]
    loaded = [pltpu.VMEM((length, widths[0]), jnp.int32)] * 2
    loaded += [pltpu.VMEM((widths[1], length), jnp.int32)] * 2
    return pl.pallas_call(
        functools.partial(first_kernel, early, kinds, columns),
        out_shape=[jax.ShapeDtypeStruct((widths[0] * kinds, columns), jnp.bfloat16)] + rows,
        in_specs=[SMEM] + [HBM] * 4,
        out_specs=[VMEM] * 5,
        scratch_shapes=loaded + [pltpu.SemaphoreType.DMA((4,))],
        compiler_params=pltpu.CompilerParams(vmem_limit_bytes=8 << 20),
        cost_estimate=count_cost(early, depth, kinds, columns),
        name="first_counts",
    )(member, *in_place(lists))


def count_cost(boxes, depth, kinds, columns):
    return pl.CostEstimate(
        flops=8 * boxes * depth * kinds * columns,
        bytes_accessed=boxes * kinds * columns * 2,
        transcendentals=0,
    )


def count_kernel(levels, kinds, columns, *refs):
    for level, (first, width) in enumerate(levels):
        rows = refs[2 * level : 2 * level + 2]
        out_ref = refs[level - len(levels)]
        count_boxes(*rows, first, width, kinds, columns, out_ref)


def count_entries(rows, levels, kinds, columns, after=(), onto=()):
    boxes = [first + width for first, width in levels]
    operands = [*rows, *after, *onto]
    return pl.pallas_call(
        functools.partial(count_kernel, levels, kinds, columns),
        out_shape=[jax.ShapeDtypeStruct((each * kinds, columns), jnp.bfloat16) for each in boxes],
        in_specs=[VMEM] * len(operands),
        out_specs=[VMEM] * len(boxes),
        input_output_aliases={len(operands) - 1: 0} if onto else {},
        compiler_params=pltpu.CompilerParams(vmem_limit_bytes=8 << 20),
        cost_estimate=count_cost(sum(boxes), rows[0].shape[1], kinds, columns),
        name="counts",
    )(*operands)


def contract(tint, count_ref, blocks, begin, kinds, ops_ref, grouped, total):
    boxes, coef = total.shape
    pitch = grouped.shape[0] // boxes
    for start in range(0, boxes, WINDOW):
        count = min(WINDOW, boxes - start)
        at = begin + start
        rows = slice(at, at + WINDOW)
        nearby = [blocks[0][rows, :]]
        for bit in range(len(HOPS[0])):
            first, second = (blocks[1 + order.index(bit)] for order in (HOPS if bit == 0 else HOPS[::-1]))
            piece = first[rows, :]
            if second is not first:
                piece = jnp.where(tint == 1, second[rows, :], piece)
            nearby.append(piece)
        nearby = jnp.concatenate(nearby, 0)
        values = jnp.dot(
            count_ref[start * kinds : (start + count) * kinds, :],
            nearby,
            preferred_element_type=jnp.float32,
        )
        for box in range(count):
            row = (start + box) * pitch
            grouped[row : row + kinds, :] = values[box * kinds : (box + 1) * kinds]

    step = 8
    for at in range(0, kinds, step):
        picked = [
            grouped[pl.ds(at + k, boxes, stride=pitch), :].astype(jnp.bfloat16)
            for k in range(step)
        ]
        term = jnp.dot(
            jnp.concatenate(picked, 1),
            ops_ref[at * coef : (at + step) * coef, :],
            preferred_element_type=jnp.float32,
        )
        total[...] = term + total[...] if at else term


def contract_scratch(boxes, kinds, coef):
    return [pltpu.VMEM((boxes * (kinds + 4), coef), jnp.float32), pltpu.VMEM((boxes, coef), jnp.float32)]


def far_kernel(kinds, tint_ref, count_ref, *refs):
    blocks = refs[:5]
    ops_ref, out_ref, grouped, total = refs[5:]
    contract(tint_ref[0], count_ref, blocks, 0, kinds, ops_ref, grouped, total)
    out_ref[...] = total[...].astype(out_ref.dtype)


def far_of(tint, counted, blocks, flat_ops, boxes, kinds):
    coef = flat_ops.shape[1]
    return pl.pallas_call(
        functools.partial(far_kernel, kinds),
        out_shape=jax.ShapeDtypeStruct((boxes, coef), jnp.bfloat16),
        in_specs=[SMEM] + [VMEM] * 7,
        out_specs=VMEM,
        scratch_shapes=contract_scratch(boxes, kinds, coef),
        compiler_params=pltpu.CompilerParams(vmem_limit_bytes=14 << 20),
        cost_estimate=pl.CostEstimate(
            flops=8 * boxes * kinds * coef * 256,
            bytes_accessed=boxes * kinds * coef * 4,
            transcendentals=0,
        ),
        name="far",
    )(tint, counted, *blocks, flat_ops)


def slots_of(basis_ref, counts_ref, box, local):
    count, coef = local.shape
    slots = basis_ref.shape[1]
    pairs = count // 2
    odd = lax.broadcasted_iota(jnp.int32, local.shape, 0) % 2
    zero = jnp.zeros_like(local)
    right = jnp.concatenate(
        [jnp.where(odd == 0, local, zero), jnp.where(odd == 1, local, zero)], 1
    )
    left = basis_ref[pl.ds(box, count)].reshape(pairs, 2, slots, coef)
    left = jnp.concatenate([left[:, 0], left[:, 1]], 2).reshape(pairs * slots, 2 * coef)
    values = lax.dot_general(
        left, right, (((1,), (1,)), ((), ())), preferred_element_type=jnp.float32
    ).reshape(pairs, slots, count)
    lane = lax.broadcasted_iota(jnp.int32, (slots, count), 1) // 2
    summed = jnp.zeros((slots, count), jnp.float32)
    for pair in range(pairs):
        summed += jnp.where(lane == pair, values[pair], 0.0)
    slot = lax.broadcasted_iota(jnp.int32, summed.shape, 0)
    limit = counts_ref[:, pl.ds(box, count)]
    return jnp.where(slot < limit, summed, 0.0)


def evaluate(far, moved, basis_ref, counts_ref, first):
    whole = moved + far.astype(jnp.float32)
    keep = lax.broadcasted_iota(jnp.int32, whole.shape, 1) < NTERMS
    local = jnp.where(keep, whole, 0.0).astype(jnp.bfloat16)
    width = local.shape[0]
    pieces = []
    for piece in range(0, width, LANES):
        box = pl.multiple_of(first + piece, LANES)
        pieces.append(slots_of(basis_ref, counts_ref, box, local[piece : piece + LANES]))
    return jnp.concatenate(pieces, 1)


def own_kernel(kinds, fine, member_ref, tint_ref, count_ref, *refs):
    blocks = refs[:5]
    (ops_ref, coarse_ref, shift_ref, far_ref, basis_ref, counts_ref) = refs[5:11]
    out_ref, rest_ref, grouped, total, moved = refs[11:]
    contract(tint_ref[0], count_ref, blocks, fine, kinds, ops_ref, grouped, total)
    parent_local = (coarse_ref[...] + total[...]).astype(jnp.bfloat16)
    parents = parent_local.shape[0]
    octants = shift_ref.shape[0]
    for octant in range(octants):
        moved[pl.ds(octant, parents, stride=octants), :] = jnp.dot(
            parent_local, shift_ref[octant], preferred_element_type=jnp.float32
        )
    width = far_ref.shape[0]
    first = pl.multiple_of(member_ref[0] * width, LANES)
    out_ref[...] = evaluate(
        far_ref[...], moved[pl.ds(first, width), :], basis_ref, counts_ref, first
    )
    rest = rest_ref.shape[0]
    rest_ref[...] = moved[pl.ds(pl.multiple_of((1 - member_ref[0]) * rest, LANES), rest), :]


def own_of(member, tint, counted, blocks, fine, flat_ops, coarse, shift, far, basis, counts, kinds, rest):
    slots, coef = basis.shape[1:]
    parents = coarse.shape[0]
    return pl.pallas_call(
        functools.partial(own_kernel, kinds, fine),
        out_shape=[
            jax.ShapeDtypeStruct((slots, far.shape[0]), jnp.float32),
            jax.ShapeDtypeStruct((rest, coef), jnp.float32),
        ],
        in_specs=[SMEM] * 2 + [VMEM] * 12,
        out_specs=[VMEM, VMEM],
        scratch_shapes=contract_scratch(parents, kinds, coef)
        + [pltpu.VMEM((parents * shift.shape[0], coef), jnp.float32)],
        compiler_params=pltpu.CompilerParams(vmem_limit_bytes=16 << 20),
        cost_estimate=pl.CostEstimate(
            flops=8 * parents * kinds * coef * 256,
            bytes_accessed=parents * kinds * coef * 4,
            transcendentals=0,
        ),
        name="own",
    )(member, tint, counted, *blocks, flat_ops, coarse, shift, far, basis, counts)


def other_kernel(member_ref, far_ref, moved_ref, basis_ref, counts_ref, own_ref, out_ref):
    width = far_ref.shape[0]
    out_ref[:, pl.ds(pl.multiple_of(member_ref[0] * width, LANES), width)] = own_ref[...]
    first = pl.multiple_of((1 - member_ref[0]) * width, LANES)
    out_ref[:, pl.ds(first, width)] = evaluate(
        far_ref[...], moved_ref[...], basis_ref, counts_ref, first
    )


def other_of(member, far, moved, basis, counts, own):
    slots = basis.shape[1]
    return pl.pallas_call(
        other_kernel,
        out_shape=jax.ShapeDtypeStruct((slots, basis.shape[0]), jnp.float32),
        in_specs=[SMEM] + [VMEM] * 5,
        out_specs=VMEM,
        compiler_params=pltpu.CompilerParams(vmem_limit_bytes=16 << 20),
        cost_estimate=pl.CostEstimate(
            flops=2 * far.shape[0] * slots * 256 * 128,
            bytes_accessed=far.shape[0] * slots * 256,
            transcendentals=0,
        ),
        name="other",
    )(member, far, moved, basis, counts, own)


def body(
    fine_parts,
    parent_parts,
    coarse_local,
    fine_source,
    fine_operator,
    parent_source,
    parent_operator,
    operators,
    child_shift,
    basis,
    counts,
):
    group = lax.axis_size("batch")
    member = lax.axis_index("batch")
    kinds, coef, _ = operators.shape
    fine_total, parent_total = fine_source.shape[1], parent_source.shape[1]
    fine = fine_total // group
    widths = (fine, parent_total)
    index = member.astype(jnp.int32).reshape(1)
    tint = colour(lax.axis_index("space")).astype(jnp.int32).reshape(1)
    lists = (fine_source, fine_operator, parent_source.T, parent_operator.T)
    special = group == 2 and fine % (8 * WINDOW) == 0

    def share(whose):
        fine_at = whose * fine // WINDOW * WINDOW
        mine = lax.dynamic_slice_in_dim(fine_parts[0], fine_at, max(fine, WINDOW), 0)
        return jnp.concatenate([mine, parent_parts[0]], 0)

    columns = 5 * WINDOW
    length = fine_source.shape[0]
    if special:
        mine, theirs = pack(index, tint, fine_parts, parent_parts, widths)
        early = fine // 2
        summed = mine.astype(jnp.float32) + rotate(theirs, "batch", 1).astype(jnp.float32)
        own = summed.astype(jnp.bfloat16)
        counted, *rows = first_counts(index, lists, widths, early, kinds, columns)
        levels = ((early, fine - early), (0, parent_total))
        counted = count_entries(rows, levels, kinds, columns, (own,), (counted,))
    else:
        summed = share(member).astype(jnp.float32)
        for step in range(1, group):
            summed += rotate(share((member + step) % group), "batch", step).astype(jnp.float32)
        own = summed.astype(jnp.bfloat16)
        fine_lists = [
            lax.dynamic_slice_in_dim(each.T, member * fine, fine, 0) for each in lists[:2]
        ]
        rows = [
            jnp.pad(
                each.astype(jnp.float32),
                ((0, 0), (0, round_up(length, LANES) - length)),
                constant_values=-1,
            )
            for each in (*fine_lists, *lists[2:])
        ]
        counted = count_entries(rows, ((0, fine), (0, parent_total)), kinds, columns)
    fine_counted, parent_counted = counted
    blocks = [own]
    for hop in range(len(HOPS[0])):
        blocks.append(hop_to_partner(own, "space", hop))
    flat_ops = operators.reshape(kinds * coef, coef)
    far = far_of(tint, fine_counted, blocks, flat_ops, fine, kinds)
    fine_rows = max(fine, WINDOW)
    parent_side = (tint, parent_counted, blocks, fine_rows, flat_ops, coarse_local, child_shift)
    if special:
        other = rotate(far, "batch", 1)
        mine, moved = own_of(index, *parent_side, far, basis, counts, kinds, fine)
        return other_of(index, other, moved, basis, counts, mine)
    gathered = jnp.zeros((fine_total, coef), far.dtype)
    for step in range(group):
        piece = rotate(far, "batch", step) if step else far
        at = (member - step) % group * fine
        gathered = lax.dynamic_update_slice_in_dim(gathered, piece, at, 0)
    values, _ = own_of(index * 0, *parent_side, gathered, basis, counts, kinds, LANES)
    return values


def solution(mesh):
    placed = (
        P("batch", "space", None),
        P("batch", "space", None),
        P("space", None),
        P(None, "space"),
        P(None, "space"),
        P(None, "space"),
        P(None, "space"),
        P(),
        P(),
        P("space", "batch", None),
        P("batch", "space"),
    )

    return jax.shard_map(
        body, mesh=mesh, in_specs=placed, out_specs=P("batch", "space"), check_vma=False
    )
```
